32 devices in a mesh: node: 8 (over z, core), local: 4 (over y, x).
Axes of the slice: x: 2, y: 2, z: 4, core: 2. Of those that a mesh axis runs over, the one named last changes fastest.
Arguments:
- tokens: bfloat16 [512, 4096], P('local', 'node'), may hold values from -6 to 6
- cotangent: bfloat16 [512, 14336], P('local', 'node'), may hold values from -0.25 to 0.25
- gate_weight: bfloat16 [4096, 14336], P('local', 'node'), may hold values from -0.09375 to 0.09375
- up_weight: bfloat16 [4096, 14336], P('local', 'node'), may hold values from -0.09375 to 0.09375
- gate_first: bfloat16 [4096, 14336], P('local', 'node'), may hold values from -3 to 3
- up_first: bfloat16 [4096, 14336], P('local', 'node'), may hold values from -3 to 3
- gate_second: bfloat16 [4096, 14336], P('local', 'node'), may hold values from 0.00029945374 to 0.029907227
- up_second: bfloat16 [4096, 14336], P('local', 'node'), may hold values from 0.00029945374 to 0.029907227
Outputs:
- input_grad: bfloat16 [512, 4096], P('local', 'node')
- gate_new: bfloat16 [4096, 14336], P('local', 'node')
- up_new: bfloat16 [4096, 14336], P('local', 'node')
- gate_first_new: bfloat16 [4096, 14336], P('local', 'node')
- up_first_new: bfloat16 [4096, 14336], P('local', 'node')
- gate_second_new: bfloat16 [4096, 14336], P('local', 'node')
- up_second_new: bfloat16 [4096, 14336], P('local', 'node')
The draws below stay inside these ranges and needn't reach their ends.
All inputs are finite; a program needn't handle non-finite values.
Results may differ from the reference program's by a relative error of at most 0.0049.
Values may be sent and summed in bfloat16 or wider, within the bound.
No kernel may reach another device: no remote copies, remote signals or barrier semaphores. Data moves between devices by JAX's collectives and lax.ppermute only.
A program may use at most 128 MiB of HBM per device.

```python
import math
import jax
import jax.numpy as jnp

D = 4096
FF = 14336
TOKENS = 512


def block_levels(stream_key, extent, split, low, high):
    def one(axis_at, parts):
        steps = jax.random.uniform(jax.random.fold_in(jax.random.fold_in(stream_key, 6), axis_at), (parts,), jnp.float32, low / len(split), high / len(split))
        return jnp.repeat(jnp.exp(steps), extent[axis_at] // parts).reshape((-1,) + (1,) * (len(extent) - axis_at - 1))

    gain = one(*split[0])
    for cut in split[1:]:
        gain = gain * one(*cut)
    return gain


def normal_values(stream_key, shape, deviation, most, split=(), held_as=jnp.bfloat16):
    level = block_levels(stream_key, shape, split, -0.22, 0.18) if split else 1.0
    result = jax.random.normal(stream_key, shape, jnp.float32) * deviation * level
    return jnp.minimum(jnp.maximum(result, -most), most).astype(held_as)


def setup_inputs(seed: int = 0) -> dict:
    streams_of = jax.random.split(jax.random.key(seed), 9)
    return {
        "tokens": normal_values(streams_of[0], (TOKENS, D), 1.0, 6.0, ((0, 4), (1, 8))),
        "cotangent": normal_values(streams_of[1], (TOKENS, FF), TOKENS ** -0.5, 0.25, ((0, 4), (1, 8))),
        "gate_weight": normal_values(streams_of[2], (D, FF), D ** -0.5, 0.09375, ((0, 4), (1, 8))),
        "up_weight": normal_values(streams_of[3], (D, FF), D ** -0.5, 0.09375, ((0, 4), (1, 8))),
        "gate_first": normal_values(streams_of[4], (D, FF), 0.5, 3.0, ((0, 4), (1, 8))),
        "up_first": normal_values(streams_of[5], (D, FF), 0.5, 3.0, ((0, 4), (1, 8))),
        "gate_second": jnp.clip(jnp.exp(math.log(0.029907227) - 4.6038955 * jax.random.uniform(streams_of[6], (D, FF), jnp.float32) ** block_levels(streams_of[6], (D, FF), ((0, 4), (1, 8)), -0.2, 0.2)), 0.00029945374, 0.029907227).astype(jnp.bfloat16),
        "up_second": jnp.clip(jnp.exp(math.log(0.029907227) - 4.6038955 * jax.random.uniform(streams_of[7], (D, FF), jnp.float32) ** block_levels(streams_of[7], (D, FF), ((0, 4), (1, 8)), -0.2, 0.2)), 0.00029945374, 0.029907227).astype(jnp.bfloat16),
    }


first_decay = 0.9
second_decay = 0.999
learn_rate = 0.001
adam_eps = 1e-08
step_count = 10

def adam_update(weight, first, second, grad):
    first_new = first_decay * first.astype(jnp.float32) + (1.0 - first_decay) * grad
    second_new = second_decay * second.astype(jnp.float32) + (1.0 - second_decay) * grad * grad
    first_hat = first_new / (1.0 - first_decay ** step_count)
    second_hat = second_new / (1.0 - second_decay ** step_count)
    weight_new = weight.astype(jnp.float32) - learn_rate * first_hat / (jnp.sqrt(second_hat) + adam_eps)
    return (weight_new.astype(jnp.bfloat16), first_new.astype(jnp.bfloat16), second_new.astype(jnp.bfloat16))

def reference(tokens, cotangent, gate_weight, up_weight, gate_first, up_first, gate_second, up_second):
    gate_pre = jnp.dot(tokens, gate_weight, preferred_element_type=jnp.float32)
    up_pre = jnp.dot(tokens, up_weight, preferred_element_type=jnp.float32)
    sigmoid_gate = jax.nn.sigmoid(gate_pre)
    upstream = cotangent.astype(jnp.float32)
    gate_grad = (upstream * up_pre * sigmoid_gate * (1.0 + gate_pre * (1.0 - sigmoid_gate))).astype(jnp.bfloat16)
    up_grad = (upstream * gate_pre * sigmoid_gate).astype(jnp.bfloat16)
    input_grad = jnp.dot(gate_grad, gate_weight.T, preferred_element_type=jnp.float32)
    input_grad = input_grad + jnp.dot(up_grad, up_weight.T, preferred_element_type=jnp.float32)
    gate_wgrad = jnp.dot(tokens.T, gate_grad, preferred_element_type=jnp.float32)
    up_wgrad = jnp.dot(tokens.T, up_grad, preferred_element_type=jnp.float32)
    gate_new, gate_first_new, gate_second_new = adam_update(gate_weight, gate_first, gate_second, gate_wgrad)
    up_new, up_first_new, up_second_new = adam_update(up_weight, up_first, up_second, up_wgrad)
    return (input_grad.astype(jnp.bfloat16), gate_new, up_new, gate_first_new, up_first_new, gate_second_new, up_second_new)
```

```python
import functools

import jax
import jax.numpy as jnp
from jax import lax
from jax.experimental import pallas as pl
from jax.experimental.pallas import tpu as pltpu
from jax.sharding import PartitionSpec as P


first_decay = 0.9
second_decay = 0.999
learn_rate = 0.001
adam_eps = 1e-08
step_count = 10

first_scale = 1.0 - first_decay**step_count
second_scale = 1.0 - second_decay**step_count
folded_rate = learn_rate * second_scale**0.5 / first_scale
folded_eps = adam_eps * second_scale**0.5

VMEM_LIMIT = 60 * 1024 * 1024
BF16 = jnp.bfloat16
F32 = jnp.float32


def cost(flops, nbytes):
    return pl.CostEstimate(flops=flops, bytes_accessed=nbytes, transcendentals=0)


def forward_kernel(slots, gate_keep, up_keep, cols_ref, gate_ref, up_ref, *outs):
    cols = cols_ref[...]
    rows = cols.shape[0] // slots
    for at, weight in ((0, gate_ref), (slots, up_ref)):
        part = jnp.dot(cols, weight[...], preferred_element_type=F32)
        for k in range(slots):
            ref = outs[at + k]
            ref[...] = part[k * rows : (k + 1) * rows].astype(ref.dtype)


def forward(slots, gate_keep, up_keep, cols, gate_weight, up_weight, block, start, count):
    tokens, depth = cols.shape
    rows = tokens // slots
    wide = block * count
    kinds = [F32 if k in gate_keep else BF16 for k in range(slots)]
    kinds += [F32 if k in up_keep else BF16 for k in range(slots)]
    weight_spec = pl.BlockSpec((depth, block), lambda j: (0, start + j))
    outs = pl.pallas_call(
        functools.partial(forward_kernel, slots, gate_keep, up_keep),
        grid=(count,),
        in_specs=[pl.BlockSpec((tokens, depth), lambda j: (0, 0)), weight_spec, weight_spec],
        out_specs=[pl.BlockSpec((rows, block), lambda j: (0, j)) for _ in kinds],
        out_shape=[jax.ShapeDtypeStruct((rows, wide), kind) for kind in kinds],
        compiler_params=pltpu.CompilerParams(vmem_limit_bytes=VMEM_LIMIT),
        cost_estimate=cost(4 * tokens * depth * wide, 4 * depth * wide + 6 * tokens * wide),
        name="forward_part",
    )(cols, gate_weight, up_weight)
    return list(outs[:slots]), list(outs[slots:])


def input_kernel(slots, has_prior, *refs):
    gates, ups = refs[:slots], refs[slots : 2 * slots]
    gate_ref, up_ref = refs[2 * slots : 2 * slots + 2]
    out_ref = refs[-1]
    across = (((1,), (1,)), ((), ()))
    gate = jnp.concatenate([ref[...] for ref in gates], axis=0)
    up = jnp.concatenate([ref[...] for ref in ups], axis=0)
    part = lax.dot_general(gate, gate_ref[...], across, preferred_element_type=F32)
    part += lax.dot_general(up, up_ref[...], across, preferred_element_type=F32)

    @pl.when(pl.program_id(0) == 0)
    def _():
        out_ref[...] = part + refs[-2][...] if has_prior else part

    @pl.when(pl.program_id(0) > 0)
    def _():
        out_ref[...] += part


def input_part(slots, gates, ups, gate_weight, up_weight, prior, block, start, count):
    rows = gates[0].shape[0]
    depth = gate_weight.shape[0]
    tokens = rows * slots
    wide = block * count
    grad_spec = pl.BlockSpec((rows, block), lambda j: (0, j))
    weight_spec = pl.BlockSpec((depth, block), lambda j: (0, start + j))
    whole = pl.BlockSpec((tokens, depth), lambda j: (0, 0))
    has_prior = prior is not None
    return pl.pallas_call(
        functools.partial(input_kernel, slots, has_prior),
        grid=(count,),
        in_specs=[grad_spec] * (2 * slots) + [weight_spec] * 2 + [whole] * has_prior,
        out_specs=whole,
        out_shape=jax.ShapeDtypeStruct((tokens, depth), F32),
        compiler_params=pltpu.CompilerParams(vmem_limit_bytes=VMEM_LIMIT),
        cost_estimate=cost(4 * tokens * depth * wide, 4 * depth * wide + 8 * tokens * depth),
        name="input_part",
    )(*gates, *ups, gate_weight, up_weight, *([prior] if has_prior else []))


def adam_kernel(slots, tile, turned_ref, *refs):
    gates, ups = refs[:slots], refs[slots : 2 * slots]
    states = refs[2 * slots : 2 * slots + 6]
    outs = refs[-6:]
    depth = turned_ref.shape[0]
    for grads, (weight_ref, first_ref, second_ref), (weight_out, first_out, second_out) in (
        (gates, states[:3], outs[:3]),
        (ups, states[3:], outs[3:]),
    ):
        grad_all = jnp.concatenate([ref[...] for ref in grads], axis=0)
        for at in range(0, depth, tile):
            here = slice(at, at + tile)
            grad = jnp.dot(turned_ref[here, :], grad_all, preferred_element_type=F32)
            first = first_decay * first_ref[here, :].astype(F32) + (1.0 - first_decay) * grad
            second = second_decay * second_ref[here, :].astype(F32) + (
                (1.0 - second_decay) * grad
            ) * grad
            root = second * lax.rsqrt(second) + folded_eps
            step = (folded_rate * first) * lax.rsqrt(root * root)
            weight_out[here, :] = (weight_ref[here, :].astype(F32) - step).astype(BF16)
            first_out[here, :] = first.astype(BF16)
            second_out[here, :] = second.astype(BF16)


def adam(slots, turned, gates, ups, states, prior, block, start, count):
    rows = gates[0].shape[0]
    depth, tokens = turned.shape
    wide = block * count
    grad_spec = pl.BlockSpec((rows, block), lambda j: (0, j))
    state_spec = pl.BlockSpec((depth, block), lambda j: (0, start + j))
    prior = list(prior)
    n_in = 1 + 2 * slots + 6
    return pl.pallas_call(
        functools.partial(adam_kernel, slots, min(depth, 128)),
        grid=(count,),
        in_specs=[pl.BlockSpec((depth, tokens), lambda j: (0, 0))]
        + [grad_spec] * (2 * slots)
        + [state_spec] * 6
        + [pl.BlockSpec(memory_space=pl.ANY)] * len(prior),
        out_specs=[state_spec] * 6,
        out_shape=[jax.ShapeDtypeStruct(states[0].shape, BF16)] * 6,
        input_output_aliases={n_in + i: i for i in range(len(prior))},
        compiler_params=pltpu.CompilerParams(vmem_limit_bytes=VMEM_LIMIT),
        cost_estimate=cost(4 * tokens * depth * wide, 24 * depth * wide),
        name="adam_part",
    )(turned, *gates, *ups, *states, *prior)


def butterfly(blocks, shift):
    bit = 1
    while bit < len(blocks):
        odd = (shift & bit) != 0
        blocks = [jnp.where(odd, blocks[j ^ bit], blocks[j]) for j in range(len(blocks))]
        bit *= 2
    return blocks


def bases(size):
    steps = []
    while (1 << len(steps)) < size:
        steps.append(1 << len(steps))
    return steps, steps[::-1]


def ring_basis(size):
    steps, _ = bases(size)
    return [3 if step == 2 else step for step in steps]


def span(steps):
    found = [0]
    for step in steps:
        found += [step ^ k for k in found]
    return found


def kept_after(steps):
    return set(span(steps[1:])) if steps else {0}


def scatter_sum(parts, steps, send):
    terms = {k: [part] for k, part in enumerate(parts)}
    for at, step in enumerate(steps):
        later = span(steps[at + 1 :])
        for k in reversed(later):
            mine = terms[k ^ step]
            total = mine[0] if len(mine) == 1 else sum(t.astype(F32) for t in mine)
            terms[k].append(send(total.astype(BF16), step))
    return terms[0]


def gather(own, steps, send):
    held = {0: own}
    for step in steps:
        for k in list(held):
            held[k ^ step] = send(held[k], step)
    return [held[k] for k in range(len(held))]


def chunks_of(blocks):
    if blocks < 3:
        return [(0, blocks)]
    head = (blocks + 1) // 2
    return [(0, head), (head, blocks - head)]


def shards(n_local, n_node, tokens, cotangent, gate_weight, up_weight, gate_first, up_first, gate_second, up_second):
    cores = n_node // n_local
    local, node = lax.axis_index("local"), lax.axis_index("node")
    layer, core = node // cores, node % cores

    def send_local(x, step):
        return lax.ppermute(x, "local", [(i, i ^ step) for i in range(n_local)])

    def send_layer(x, step):
        return lax.ppermute(x, "node", [(i, i ^ (step * cores)) for i in range(n_node)])

    def send_core(x, step):
        return lax.ppermute(x, "node", [(i, i ^ step) for i in range(n_node)])

    order, reverse = bases(n_local)
    ring = ring_basis(n_local)
    core_order, _ = bases(cores)

    gathered = gather(tokens, ring, send_layer)
    picked = butterfly(gathered, layer ^ local)
    half = [picked[0]] + [send_local(picked[k], k) for k in range(1, n_local)]
    half = jnp.concatenate(half, axis=0)
    cols = jnp.concatenate(butterfly(gather(half, core_order, send_core), core), axis=1)
    turned = cols.T

    width = gate_weight.shape[1]
    block = 256 if width % 256 == 0 else width
    states = [gate_weight, gate_first, gate_second, up_weight, up_first, up_second]
    slots = n_local
    updated, partial_sum = [], None
    for start, count in chunks_of(width // block):
        here = slice(start * block, (start + count) * block)
        gate_parts, up_parts = forward(
            slots, kept_after(order), kept_after(reverse), cols, gate_weight, up_weight, block, start, count
        )
        gate_pre = sum(t.astype(F32) for t in scatter_sum(gate_parts, order, send_local))
        up_pre = sum(t.astype(F32) for t in scatter_sum(up_parts, reverse, send_local))
        upstream = cotangent[:, here].astype(F32)
        sigmoid_gate = jax.nn.sigmoid(gate_pre)
        gate_grad = (upstream * up_pre * sigmoid_gate * (1.0 + gate_pre * (1.0 - sigmoid_gate))).astype(BF16)
        up_grad = (upstream * gate_pre * sigmoid_gate).astype(BF16)
        gates = gather(gate_grad, reverse, send_local)
        ups = gather(up_grad, order, send_local)
        partial_sum = input_part(slots, gates, ups, gate_weight, up_weight, partial_sum, block, start, count)
        updated = adam(slots, turned, gates, ups, states, updated, block, start, count)

    rows, wide = tokens.shape
    pieces = [partial_sum[:, i * wide : (i + 1) * wide] for i in range(cores)]
    summed = sum(t.astype(F32) for t in scatter_sum(butterfly(pieces, core), core_order, send_core))
    by_slot = [summed[k * rows : (k + 1) * rows] for k in range(n_local)]
    mine = sum(t.astype(F32) for t in scatter_sum(butterfly(by_slot, layer), ring, send_layer))
    home = []
    for a in range(n_node):
        for b in range(n_local):
            to_node, to_local = b * cores + a % cores, b ^ (a // cores)
            home.append((a * n_local + b, to_node * n_local + to_local))
    input_grad = lax.ppermute(mine.astype(BF16), ("node", "local"), home)

    gate_new, gate_first_new, gate_second_new, up_new, up_first_new, up_second_new = updated
    return (
        input_grad,
        gate_new,
        up_new,
        gate_first_new,
        up_first_new,
        gate_second_new,
        up_second_new,
    )


def solution(mesh):
    n_local, n_node = mesh.shape["local"], mesh.shape["node"]
    if n_node % n_local or n_local & (n_local - 1) or n_node & (n_node - 1):
        raise ValueError("unsupported mesh")
    spec = P("local", "node")
    return jax.shard_map(
        functools.partial(shards, n_local, n_node),
        mesh=mesh,
        in_specs=(spec,) * 8,
        out_specs=(spec,) * 7,
        check_vma=False,
    )
```

```python
import functools

import jax
import jax.numpy as jnp
from jax import lax
from jax.experimental import pallas as pl
from jax.experimental.pallas import tpu as pltpu
from jax.sharding import PartitionSpec as P


first_decay = 0.9
second_decay = 0.999
learn_rate = 0.001
adam_eps = 1e-08
step_count = 10

first_scale = 1.0 - first_decay**step_count
second_scale = 1.0 - second_decay**step_count
folded_rate = learn_rate * second_scale**0.5 / first_scale
folded_eps = adam_eps * second_scale**0.5

MIB = 1024 * 1024
BF16 = jnp.bfloat16
F32 = jnp.float32


def cost(flops, nbytes):
    return pl.CostEstimate(flops=int(flops), bytes_accessed=int(nbytes), transcendentals=0)


def params(mib):
    return pltpu.CompilerParams(vmem_limit_bytes=mib * MIB)


def steps_of(size):
    steps = []
    while (1 << len(steps)) < size:
        steps.append(1 << len(steps))
    return steps


def span(steps):
    found = [0]
    for step in steps:
        found += [step ^ k for k in found]
    return found


def arrange(steps):
    if not steps:
        return [0]
    rest = arrange(steps[1:])
    return [k ^ steps[0] for k in rest] + rest


def assemble_kernel(slots, where_ref, mine_ref, far_ref, swap_mine_ref, swap_far_ref, cols_ref):
    layer, core = where_ref[0], where_ref[1]
    rows, wide = mine_ref.shape[1:]
    at = 0
    for k in range(slots):
        j = layer ^ k
        odd, q = j & 1, j >> 1
        own = jnp.where(odd == 0, mine_ref[q], far_ref[q])
        other = jnp.where(odd == 0, swap_mine_ref[q], swap_far_ref[q])
        here = slice(k * rows, (k + 1) * rows)
        cols_ref[here, :wide] = jnp.where(core == 0, own, other)
        cols_ref[here, wide:] = jnp.where(core == 0, other, own)


def forward_kernel(slots, order, cols_ref, weight_ref, send_ref, keep_ref):
    part = jnp.dot(cols_ref[...], weight_ref[...], preferred_element_type=F32)
    rows = cols_ref.shape[0] // slots
    half = slots // 2
    for at, k in enumerate(order):
        piece = part[k * rows : (k + 1) * rows]
        if at < half:
            send_ref[at * rows : (at + 1) * rows] = piece.astype(BF16)
        else:
            keep_ref[(at - half) * rows : (at - half + 1) * rows] = piece


def forward(slots, steps, cols, weight, block):
    tokens, depth = cols.shape
    width = weight.shape[1]
    out_spec = pl.BlockSpec((tokens // 2, block), lambda j: (0, j))
    return pl.pallas_call(
        functools.partial(forward_kernel, slots, arrange(steps)),
        grid=(width // block,),
        in_specs=[pl.BlockSpec((tokens, depth), lambda j: (0, 0)), pl.BlockSpec((depth, block), lambda j: (0, j))],
        out_specs=[out_spec, out_spec],
        out_shape=[
            jax.ShapeDtypeStruct((tokens // 2, width), BF16),
            jax.ShapeDtypeStruct((tokens // 2, width), F32),
        ],
        compiler_params=params(16),
        cost_estimate=cost(2 * tokens * depth * width, 2 * depth * width + 3 * tokens * width),
        name="forward_part",
    )(cols, weight)


def grads_kernel(n_terms, *refs):
    gate_terms, up_terms = refs[:n_terms], refs[n_terms : 2 * n_terms]
    upstream_ref, out_ref = refs[-2:]
    gate_pre = sum(ref[...].astype(F32) for ref in gate_terms)
    up_pre = sum(ref[...].astype(F32) for ref in up_terms)
    upstream = upstream_ref[...].astype(F32)
    sigmoid_gate = jax.nn.sigmoid(gate_pre)
    scaled = upstream * sigmoid_gate
    out_ref[0] = (scaled * up_pre * (1.0 + gate_pre * (1.0 - sigmoid_gate))).astype(BF16)
    out_ref[1] = (scaled * gate_pre).astype(BF16)


def last_rows(array, rows, block):
    last = array.shape[0] // rows - 1
    return pl.BlockSpec((rows, block), lambda j: (last, j))


def hidden_grads(gate_terms, up_terms, cotangent, chunk, rows, block):
    width = cotangent.shape[1]
    terms = gate_terms + up_terms
    return pl.pallas_call(
        functools.partial(grads_kernel, len(gate_terms)),
        grid=(width // block,),
        in_specs=[last_rows(t, rows, block) for t in terms] + [pl.BlockSpec((rows, block), lambda j: (chunk, j))],
        out_specs=pl.BlockSpec((2, rows, block), lambda j: (0, 0, j)),
        out_shape=jax.ShapeDtypeStruct((2, rows, width), BF16),
        compiler_params=params(8),
        cost_estimate=cost(40 * rows * width, 20 * rows * width),
        name="hidden_grads",
    )(*terms, cotangent)


def grad_spec(piece, rows, block):
    array, lead = piece
    if lead is None:
        return pl.BlockSpec((rows, block), lambda j, *_: (0, j))
    return pl.BlockSpec((None, rows, block), lambda j, *_: (lead, 0, j))


def input_kernel(slots, order, where_ref, *refs):
    gates, ups = refs[:slots], refs[slots : 2 * slots]
    gate_ref, up_ref, send_ref, keep_ref, total_ref = refs[2 * slots :]
    across = (((1,), (1,)), ((), ()))
    gate = jnp.concatenate([ref[...] for ref in gates], axis=0)
    up = jnp.concatenate([ref[...] for ref in ups], axis=0)
    part = lax.dot_general(gate, gate_ref[...], across, preferred_element_type=F32)
    part += lax.dot_general(up, up_ref[...], across, preferred_element_type=F32)
    rows = gates[0].shape[0]
    step = pl.program_id(0)

    @pl.when(step == 0)
    def _():
        total_ref[...] = part

    @pl.when(step > 0)
    def _():
        total_ref[...] += part

    @pl.when(step == pl.num_programs(0) - 1)
    def _():
        layer, core = where_ref[0], where_ref[1]
        wide = total_ref.shape[1] // 2
        for at, j in enumerate(order):
            piece = total_ref[pl.ds(pl.multiple_of((layer ^ j) * rows, rows), rows), :]
            low, high = piece[:, :wide], piece[:, wide:]
            keep_ref[at * rows : (at + 1) * rows] = jnp.where(core == 0, low, high)
            send_ref[at * rows : (at + 1) * rows] = jnp.where(core == 0, high, low).astype(BF16)


def input_part(slots, order, where, gates, ups, gate_weight, up_weight, rows, block):
    depth, width = gate_weight.shape
    tokens = rows * slots
    weight_spec = pl.BlockSpec((depth, block), lambda j, *_: (0, j))
    whole = pl.BlockSpec((tokens, depth // 2), lambda j, *_: (0, 0))
    return pl.pallas_call(
        functools.partial(input_kernel, slots, order),
        grid_spec=pltpu.PrefetchScalarGridSpec(
            num_scalar_prefetch=1,
            grid=(width // block,),
            in_specs=[grad_spec(p, rows, block) for p in gates + ups] + [weight_spec] * 2,
            out_specs=[whole, whole],
            scratch_shapes=[pltpu.VMEM((tokens, depth), F32)],
        ),
        out_shape=[
            jax.ShapeDtypeStruct((tokens, depth // 2), BF16),
            jax.ShapeDtypeStruct((tokens, depth // 2), F32),
        ],
        compiler_params=params(20),
        cost_estimate=cost(4 * tokens * depth * width, 4 * depth * width),
        name="input_part",
    )(where, *[p[0] for p in gates + ups], gate_weight, up_weight)


def adam_kernel(n_grads, tile, turned_ref, *refs):
    gates, ups = refs[:n_grads], refs[n_grads : 2 * n_grads]
    states = refs[2 * n_grads : 2 * n_grads + 6]
    outs = refs[-6:]
    depth = turned_ref.shape[0]
    for grads, (weight_ref, first_ref, second_ref), (weight_out, first_out, second_out) in (
        (gates, states[:3], outs[:3]),
        (ups, states[3:], outs[3:]),
    ):
        grad_all = jnp.concatenate([ref[...] for ref in grads], axis=0)
        for at in range(0, depth, tile):
            here = slice(at, at + tile)
            grad = jnp.dot(turned_ref[here, :], grad_all, preferred_element_type=F32)
            first = first_decay * first_ref[here, :].astype(F32) + (1.0 - first_decay) * grad
            second = second_decay * second_ref[here, :].astype(F32) + ((1.0 - second_decay) * grad) * grad
            root = second * lax.rsqrt(second) + folded_eps
            step = (folded_rate * first) * lax.rsqrt(root * root)
            weight_out[here, :] = (weight_ref[here, :].astype(F32) - step).astype(BF16)
            first_out[here, :] = first.astype(BF16)
            second_out[here, :] = second.astype(BF16)


def adam(turned, gates, ups, states, rows, block):
    depth, tokens = turned.shape
    width = states[0].shape[1]
    state_spec = pl.BlockSpec((depth, block), lambda j: (0, j))
    return pl.pallas_call(
        functools.partial(adam_kernel, len(gates), min(depth, 128)),
        grid=(width // block,),
        in_specs=[pl.BlockSpec((depth, tokens), lambda j: (0, 0))]
        + [grad_spec(p, rows, block) for p in gates + ups]
        + [state_spec] * 6,
        out_specs=[state_spec] * 6,
        out_shape=[jax.ShapeDtypeStruct(states[0].shape, BF16)] * 6,
        compiler_params=params(32),
        cost_estimate=cost(4 * tokens * depth * width, 24 * depth * width),
        name="adam_part",
    )(turned, *[p[0] for p in gates + ups], *states)


def shards(n_local, n_node, tokens, cotangent, gate_weight, up_weight, gate_first, up_first, gate_second, up_second):
    local, node = lax.axis_index("local"), lax.axis_index("node")
    layer, core = node // 2, node % 2
    where = jnp.stack([layer, core]).astype(jnp.int32)
    slots = n_local

    def send_local(x, step):
        return lax.ppermute(x, "local", [(i, i ^ step) for i in range(n_local)])

    def send_node(x, step):
        return lax.ppermute(x, "node", [(i, i ^ step) for i in range(n_node)])

    def send_across(x, to):
        pairs = []
        for a in range(n_node):
            for b in range(n_local):
                to_layer, to_local = to(a // 2, b)
                pairs.append((a * n_local + b, (to_layer * 2 + a % 2) * n_local + to_local))
        return lax.ppermute(x, ("node", "local"), pairs)

    order = steps_of(n_local)
    reverse = order[::-1]
    far = [k for k in range(n_local) if k % 2 == 0]
    pairs_order = [k + 1 for k in far] + far

    width = gate_weight.shape[1]
    block = 256 if width % 256 == 0 else width
    rows = tokens.shape[0] // 2
    wide = tokens.shape[1]
    half = slots // 2

    def columns(chunk):
        here = tokens[chunk * rows : (chunk + 1) * rows]
        mine = jnp.stack([send_across(here, lambda z, l, q=q: (l ^ z ^ q, z)) for q in far])
        other = send_node(mine, 2)
        swap_mine, swap_other = send_node(mine, 1), send_node(other, 1)
        return pl.pallas_call(
            functools.partial(assemble_kernel, slots),
            in_specs=[pl.BlockSpec(memory_space=pltpu.SMEM)] + [pl.BlockSpec(memory_space=pltpu.VMEM)] * 4,
            out_specs=pl.BlockSpec(memory_space=pltpu.VMEM),
            out_shape=jax.ShapeDtypeStruct((slots * rows, 2 * wide), BF16),
            compiler_params=params(8),
            cost_estimate=cost(0, 8 * slots * rows * wide),
            name="assemble",
        )(where, mine, other, swap_mine, swap_other)

    def scatter_sum(cols, steps, weight):
        send, keep = forward(slots, steps, cols, weight, block)
        terms = [keep]
        at = half
        for i, step in enumerate(steps):
            terms.append(send_local(send, step))
            if i + 1 < len(steps):
                size = at // 2 * rows
                send = sum(t[-at * rows :][:size].astype(F32) for t in terms).astype(BF16)
                at //= 2
        return terms

    def gather(own, direct, lead, steps):
        held = {0: (own, lead)}
        for i, step in enumerate(steps):
            for k in span(steps[:i]):
                if k == 0:
                    held[step] = (direct[step], lead)
                else:
                    array, at = held[k]
                    held[k ^ step] = (send_local(array if at is None else array[at], step), None)
        return [held[k] for k in range(slots)]

    all_cols, all_gates, all_ups, input_rows = [], [], [], []
    for chunk in range(2):
        cols = columns(chunk)
        gate_terms = scatter_sum(cols, order, gate_weight)
        up_terms = scatter_sum(cols, reverse, up_weight)
        own = hidden_grads(gate_terms, up_terms, cotangent, chunk, rows, block)
        direct = {step: send_local(own, step) for step in order}
        gates = gather(own, direct, 0, reverse)
        ups = gather(own, direct, 1, order)
        send, keep = input_part(slots, pairs_order, where, gates, ups, gate_weight, up_weight, rows, block)
        summed = keep + send_node(send, 1).astype(F32)
        pieces = summed[half * rows :] + send_node(summed[: half * rows].astype(BF16), 2).astype(F32)
        pieces = pieces.astype(BF16)
        arrived = [
            send_across(pieces[i * rows : (i + 1) * rows], lambda z, l, q=q: (l, l ^ z ^ q))
            for i, q in enumerate(far)
        ]
        input_rows.append(sum(t.astype(F32) for t in arrived).astype(BF16))
        all_cols.append(cols)
        all_gates += gates
        all_ups += ups

    turned = jnp.concatenate(all_cols, axis=0).T
    states = [gate_weight, gate_first, gate_second, up_weight, up_first, up_second]
    gate_new, gate_first_new, gate_second_new, up_new, up_first_new, up_second_new = adam(
        turned, all_gates, all_ups, states, rows, block
    )
    return (
        jnp.concatenate(input_rows, axis=0),
        gate_new,
        up_new,
        gate_first_new,
        up_first_new,
        gate_second_new,
        up_second_new,
    )


def solution(mesh):
    n_local, n_node = mesh.shape["local"], mesh.shape["node"]
    if n_node != 2 * n_local or n_local < 4 or n_local & (n_local - 1):
        raise ValueError("unsupported mesh")
    spec = P("local", "node")
    return jax.shard_map(
        functools.partial(shards, n_local, n_node),
        mesh=mesh,
        in_specs=(spec,) * 8,
        out_specs=(spec,) * 7,
        check_vma=False,
    )
```
